32 devices in a mesh: tile: 8 (over z, x), seg: 4 (over y, core).
Axes of the slice: x: 2, y: 2, z: 4, core: 2. Of those that a mesh axis runs over, the one named last changes fastest.
Arguments:
- shell_state: float32 [4, 128, 64, 1024], P(None, 'tile', 'seg'), may hold values from -6 to 6
- diffusivity: float32 [128, 64, 1024], P('tile', 'seg'), may hold values from 0.02 to 0.16
- inlet_enthalpy: float32 [2048], P('tile'), may hold values from -6 to 6
- transfer_units: float32 [64, 2048], P('seg', 'tile'), as said below
- wall_cells: int32 [32, 32, 512], P(('tile', 'seg')), may hold values from 0 to 262143, as said below
- tube_slots: int32 [64, 2048], P('seg', 'tile'), may hold values from 0 to 16383, as said below
Outputs:
- shell_next: float32 [4, 128, 64, 1024], P(None, 'tile', 'seg')
- enthalpy: float32 [64, 2048], P('seg', 'tile')
The draws below stay inside these ranges and needn't reach their ends.
Inputs may be any that keep to these rules, and one draw needn't show every extreme that they name: `wall_cells`: entries are local cell numbers of the owner's block. Entry [o, d, j] is the wall cell of the tube cell of device d whose tube_slots entry is o * 512 + j; slots that no tube cell names hold arbitrary cells. `tube_slots`: each entry is o * 512 + j with o an owner device and j < 512; the entries of one device's block are distinct, so one owner serves at most 512 tube cells of one device. `transfer_units`: Positive.
All inputs are finite; a program needn't handle non-finite values.
Results may differ from the reference program's by a relative error of at most 0.00002.
Values sent between devices are 32-bit elements; how exact they have to be, the bound alone decides.
A program may use at most 128 MiB of HBM per device.

```python
import math
import jax
import jax.numpy as jnp
from jax import lax

CX = 16
CY = 16
CZ = 1024
TUBE_DEV = 256
AX_DEV = 16
NX = 128
NY = 64
NZ = 1024
TUBE_TOTAL = 2048
AXIAL_CELLS = 64
CAP = 512
N_TILE = 8
N_SEG = 4


def routing_tables(key):
    total = TUBE_DEV * AX_DEV
    devices = N_TILE * N_SEG
    rest = total - CAP
    span = (devices - 1) * (devices - 1)
    cell_count = CX * CY * CZ
    hot_key, pad_key, order_key = jax.random.split(jax.random.fold_in(key, 7), 3)
    hot_owner = jax.random.randint(hot_key, (), 0, devices)
    position = jnp.arange(total, dtype=jnp.int32)
    later_pos = jnp.maximum(position - CAP, 0)
    levels = jnp.arange(1, devices - 1, dtype=jnp.int32)
    group = jnp.sum((levels[None, :] * levels[None, :] * rest <= later_pos[:, None] * span).astype(jnp.int32), axis=1)
    group_start = (group * group * rest + span - 1) // span
    is_hot = position < CAP
    slot_within = jnp.where(is_hot, position, later_pos - group_start)

    def one_device(device_key):
        first_key, second_key, third_key = jax.random.split(device_key, 3)
        order = jax.random.permutation(first_key, devices - 1).astype(jnp.int32)
        owner_cold = (hot_owner + 1 + order[group]) % devices
        owner = jnp.where(is_hot, hot_owner, owner_cold)
        shuffle = jax.random.permutation(second_key, total).astype(jnp.int32)
        cells = jax.random.randint(third_key, (total,), 0, cell_count)
        return (owner, shuffle, cells)
    device_keys = jax.random.split(order_key, devices)
    owner, shuffle, cells = jax.vmap(one_device)(device_keys)
    rows_index = jnp.arange(devices, dtype=jnp.int32)[:, None]
    slot_value = owner * CAP + slot_within[None, :]
    tube_local = jnp.zeros((devices, total), jnp.int32).at[rows_index, shuffle].set(slot_value)
    walls = jax.random.randint(pad_key, (devices, devices, CAP), 0, cell_count)
    walls = walls.at[owner, rows_index, slot_within[None, :]].set(cells)
    return (walls, tube_local)


def draw_wall_cells(key, part):
    return routing_tables(key)[0]


def draw_tube_slots(key, part):
    tube_local = routing_tables(key)[1]
    blocks = tube_local.reshape(N_TILE, N_SEG, AX_DEV, TUBE_DEV)
    return jnp.transpose(blocks, (1, 2, 0, 3)).reshape(AXIAL_CELLS, TUBE_TOTAL)


def draw_transfer_units(key, part):
    flow_rate_key, roughness_key, surge_random_key, extent_random_key = jax.random.split(key, 4)
    flow_rate = jnp.exp(jax.random.uniform(flow_rate_key, (1, TUBE_TOTAL), jnp.float32, jnp.log(0.2 / AXIAL_CELLS), jnp.log(1.0 / 12.0)))
    roughness = jax.random.uniform(roughness_key, (AXIAL_CELLS, TUBE_TOTAL), jnp.float32, 0.5, 1.5)
    surge_rows = jax.random.bernoulli(surge_random_key, 3.0 / AXIAL_CELLS, (AXIAL_CELLS, 1)).astype(jnp.float32)
    surge_extent = jax.random.uniform(extent_random_key, (AXIAL_CELLS, TUBE_TOTAL), jnp.float32, 0.25, 0.7)
    return flow_rate * roughness + surge_rows * surge_extent


def block_scale(own_key, extent, shards, smallest, largest):
    level, own = 1.0, jax.random.fold_in(own_key, 6)
    for dim, shards_of in shards:
        heights = jnp.exp(jax.random.uniform(jax.random.fold_in(own, dim), (shards_of,), jnp.float32, smallest / len(shards), largest / len(shards)))
        level = level * jnp.repeat(heights, extent[dim] // shards_of).reshape([-1 if axis == dim else 1 for axis in range(len(extent))])
    return level


def gaussian(rng, extent, scale, limit, shards=(), held_as=jnp.bfloat16):
    entries = scale * jax.random.normal(rng, extent, jnp.float32)
    if shards:
        entries = entries * block_scale(rng, extent, shards, -0.22, 0.18)
    return jnp.clip(entries, -limit, limit).astype(held_as)


def setup_inputs(seed: int = 0) -> dict:
    key_of = jax.random.split(jax.random.key(seed), 7)
    shell_state = gaussian(key_of[0], (4, NX, NY, NZ), 1.0, 6.0, ((1, 8), (2, 4)), jnp.float32)
    diffusivity = jnp.clip(jnp.exp(math.log(0.16) - 2.0794415 * jax.random.uniform(key_of[1], (NX, NY, NZ), jnp.float32) ** block_scale(key_of[1], (NX, NY, NZ), ((0, 8), (1, 4)), -0.2, 0.2)), 0.02, 0.16)
    inlet_enthalpy = gaussian(key_of[2], (TUBE_TOTAL,), 1.0, 6.0, ((0, 8),), jnp.float32)
    transfer_units = draw_transfer_units(jax.random.fold_in(key_of[6], 71), 0)
    wall_cells = draw_wall_cells(jax.random.fold_in(key_of[6], 71), 0)
    tube_slots = draw_tube_slots(jax.random.fold_in(key_of[6], 71), 0)
    return {"shell_state": shell_state, "diffusivity": diffusivity, "inlet_enthalpy": inlet_enthalpy, "transfer_units": transfer_units, "wall_cells": wall_cells, "tube_slots": tube_slots}


DEPOSIT_SCALE = 2.0


def diffuse(state, diffusivity):
    padded = jnp.pad(state, ((0, 0), (1, 1), (1, 1), (1, 1)))
    neighbours = padded[:, 2:, 1:-1, 1:-1] + padded[:, :-2, 1:-1, 1:-1]
    neighbours = neighbours + padded[:, 1:-1, 2:, 1:-1] + padded[:, 1:-1, :-2, 1:-1]
    neighbours = neighbours + padded[:, 1:-1, 1:-1, 2:] + padded[:, 1:-1, 1:-1, :-2]
    return state + diffusivity[None] * (neighbours - 6.0 * state)


def reference(shell_state, diffusivity, inlet_enthalpy, transfer_units, wall_cells, tube_slots):
    fresh = diffuse(shell_state, diffusivity)
    axial_index = jnp.arange(AXIAL_CELLS, dtype=jnp.int32)[:, None]
    tube_index = jnp.arange(TUBE_TOTAL, dtype=jnp.int32)[None, :]
    holder = (tube_index // TUBE_DEV) * N_SEG + axial_index // AX_DEV
    owner = tube_slots // CAP
    column = tube_slots % CAP
    local_cell = wall_cells[owner, holder, column]
    plane_cells = CY * CZ
    x_cell = (owner // N_SEG) * CX + local_cell // plane_cells
    y_cell = (owner % N_SEG) * CY + (local_cell // CZ) % CY
    z_cell = local_cell % CZ
    wall_state = fresh[:, x_cell, y_cell, z_cell]
    speed_sq = wall_state[1] * wall_state[1] + wall_state[2] * wall_state[2] + wall_state[3] * wall_state[3]
    decay_rate = jnp.exp(-transfer_units * (1.0 + speed_sq) ** 0.3)
    source = (1.0 - decay_rate) * wall_state[0]

    def march(current, inputs):
        gain_row, shift_row = inputs
        updated = gain_row * current + shift_row
        return updated, (updated, updated - current)

    last_row, outputs = lax.scan(march, inlet_enthalpy, (decay_rate, source))
    enthalpy, heat_flow = outputs
    deposit = jnp.zeros((NX, NY, NZ), jnp.float32).at[x_cell, y_cell, z_cell].add(heat_flow)
    heated = fresh[0] - DEPOSIT_SCALE * deposit
    shell_next = jnp.concatenate([heated[None], fresh[1:]], axis=0)
    return shell_next, enthalpy
```

```python
import functools

import jax
import jax.numpy as jnp
from jax import lax
from jax.experimental import pallas as pl
from jax.experimental.pallas import tpu as pltpu
from jax.sharding import PartitionSpec as P

DEPOSIT_SCALE = 2.0
LANES = 128
BF16 = jnp.bfloat16
F32 = jnp.float32
VMEM_LIMIT = 56 * 1024 * 1024


def pieces_of(value, count):
    parts = []
    for _ in range(count):
        part = value.astype(BF16)
        parts.append(part)
        value = value - part.astype(F32)
    return parts


def one_hot(index_row, rows):
    rows_iota = lax.broadcasted_iota(jnp.int32, (rows, index_row.shape[1]), 0)
    return jnp.where(rows_iota == index_row, 1.0, 0.0).astype(BF16)


def halo(state):
    def send(cells, axis, step):
        count = lax.axis_size(axis)
        if step > 0:
            pairs = [(i, i + 1) for i in range(count - 1)]
        else:
            pairs = [(i + 1, i) for i in range(count - 1)]
        return lax.ppermute(cells, axis, pairs)

    x_low = send(state[:, -1], "tile", 1)
    x_high = send(state[:, 0], "tile", -1)
    y_low = send(state[:, :, -1], "seg", 1)
    y_high = send(state[:, :, 0], "seg", -1)
    return x_low, x_high, y_low, y_high


def cell_parts(cells, plane, depth):
    xy = cells // depth
    z = cells % depth
    return (z // LANES) * plane + xy, z % LANES


def serve_kernel(
    state_ref, diff_ref, xl_ref, xh_ref, yl_ref, yh_ref, cells_ref,
    fresh_ref, out_ref, speed_ref, table_ref,
):
    nx, ny, nz = diff_ref.shape
    plane = nx * ny
    chunks = nz // LANES
    step = pl.program_id(0)

    @pl.when(step == 0)
    def _():
        row = lax.broadcasted_iota(jnp.int32, (ny, nz), 0)
        col = lax.broadcasted_iota(jnp.int32, (ny, nz), 1)

        def at_x(x, below, above):
            diffusivity = diff_ref[x]
            speed = None
            for c in range(4):
                cur = state_ref[c, x]
                nbr = above(c) + below(c)
                y_up = jnp.where(row == ny - 1, yh_ref[c, pl.ds(x, 1), :], pltpu.roll(cur, ny - 1, 0))
                y_dn = jnp.where(row == 0, yl_ref[c, pl.ds(x, 1), :], pltpu.roll(cur, 1, 0))
                nbr = nbr + y_up + y_dn
                z_up = jnp.where(col == nz - 1, 0.0, pltpu.roll(cur, nz - 1, 1))
                z_dn = jnp.where(col == 0, 0.0, pltpu.roll(cur, 1, 1))
                nbr = nbr + z_up + z_dn
                new = cur + diffusivity * (nbr - 6.0 * cur)
                fresh_ref[c, x] = new
                if c == 1:
                    speed = new * new
                elif c > 1:
                    speed = speed + new * new
            speed_ref[x] = speed

        at_x(0, lambda c: xl_ref[c], lambda c: state_ref[c, 1])

        def inner(x, carry):
            at_x(x, lambda c: state_ref[c, x - 1], lambda c: state_ref[c, x + 1])
            return carry

        lax.fori_loop(1, nx - 1, inner, 0)
        at_x(nx - 1, lambda c: state_ref[c, nx - 2], lambda c: xh_ref[c])

        for k in range(chunks):
            lanes = slice(k * LANES, (k + 1) * LANES)
            rows = slice(k * plane, (k + 1) * plane)
            for c in range(2):
                source = fresh_ref.at[0] if c == 0 else speed_ref
                block = source[:, :, lanes].reshape(plane, LANES)
                for p, part in enumerate(pieces_of(block.T, 2)):
                    base = (c * 2 + p) * LANES
                    table_ref[base : base + LANES, rows] = part

    where_row, where_lane = cell_parts(cells_ref[0, pl.ds(step, 1), :], plane, nz)
    cap = where_row.shape[1]
    hot = one_hot(where_row, plane * chunks)
    lines = jnp.dot(table_ref[...], hot, preferred_element_type=F32)
    lane_iota = lax.broadcasted_iota(jnp.int32, (LANES, cap), 0)
    chosen = lane_iota == where_lane
    for c in range(2):
        both = lines[2 * c * LANES : (2 * c + 1) * LANES] + lines[(2 * c + 1) * LANES : (2 * c + 2) * LANES]
        out_ref[0, c : c + 1, :] = jnp.sum(jnp.where(chosen, both, 0.0), axis=0, keepdims=True)


def serve(state, diffusivity, halos, wall_cells):
    _, devices, cap = wall_cells.shape
    nx, ny, nz = diffusivity.shape

    def whole(shape):
        return pl.BlockSpec(shape, lambda i: (0,) * len(shape))

    return pl.pallas_call(
        serve_kernel,
        grid=(devices,),
        in_specs=[whole(a.shape) for a in (state, diffusivity, *halos, wall_cells)],
        out_specs=[whole(state.shape), pl.BlockSpec((1, 2, cap), lambda i: (i, 0, 0))],
        out_shape=[
            jax.ShapeDtypeStruct(state.shape, F32),
            jax.ShapeDtypeStruct((devices, 2, cap), F32),
        ],
        scratch_shapes=[
            pltpu.VMEM((nx, ny, nz), F32),
            pltpu.VMEM((4 * LANES, nx * ny * nz // LANES), BF16),
        ],
        compiler_params=pltpu.CompilerParams(vmem_limit_bytes=VMEM_LIMIT),
    )(state, diffusivity, *halos, wall_cells)


def slot_parts(slots, cap, devices):
    owner = slots // cap
    column = slots % cap
    return (column // LANES) * devices + owner, column % LANES


def lookup_kernel(walls_ref, slots_ref, units_ref, gain_ref, shift_ref, ends_ref, table_ref):
    devices, _, cap = walls_ref.shape
    rows, tubes = slots_ref.shape
    chunks = cap // LANES
    slot_rows = devices * chunks
    for k in range(chunks):
        for c in range(2):
            block = walls_ref[:, c, k * LANES : (k + 1) * LANES]
            for p, part in enumerate(pieces_of(block.T, 3)):
                first = p * slot_rows + k * devices
                table_ref[c * LANES : (c + 1) * LANES, first : first + devices] = part
    lane_iota = lax.broadcasted_iota(jnp.int32, (LANES, tubes), 0)
    gain = jnp.ones((1, tubes), F32)
    shift = jnp.zeros((1, tubes), F32)
    for i in range(rows):
        where_row, where_lane = slot_parts(slots_ref[i : i + 1, :], cap, devices)
        hot = one_hot(where_row, slot_rows)
        hot = jnp.concatenate([hot, hot, hot], axis=0)
        lines = jnp.dot(table_ref[...], hot, preferred_element_type=F32)
        chosen = lane_iota == where_lane
        temperature, speed = [
            jnp.sum(jnp.where(chosen, lines[c * LANES : (c + 1) * LANES], 0.0), axis=0, keepdims=True)
            for c in range(2)
        ]
        decay = jnp.exp(-units_ref[i : i + 1, :] * jnp.exp(0.3 * jnp.log(1.0 + speed)))
        source = (1.0 - decay) * temperature
        shift = decay * shift + source
        gain = decay * gain
        gain_ref[i : i + 1, :] = gain
        shift_ref[i : i + 1, :] = shift
    ends_ref[0:1, :] = gain
    ends_ref[1:2, :] = shift


def lookup(walls, slots, units):
    devices, _, cap = walls.shape
    shape = jax.ShapeDtypeStruct(slots.shape, F32)
    return pl.pallas_call(
        lookup_kernel,
        out_shape=[shape, shape, jax.ShapeDtypeStruct((2, slots.shape[1]), F32)],
        scratch_shapes=[pltpu.VMEM((2 * LANES, 3 * devices * cap // LANES), BF16)],
        compiler_params=pltpu.CompilerParams(vmem_limit_bytes=VMEM_LIMIT),
    )(walls, slots, units)


def march_kernel(seg_axis, cap, devices, ends_ref, inlet_ref, gain_ref, shift_ref, slots_ref, enthalpy_ref, out_ref):
    rows, tubes = slots_ref.shape
    chunks = cap // LANES
    slot_rows = devices * chunks
    mine = lax.axis_index(seg_axis)
    start = inlet_ref[...]
    for s in range(ends_ref.shape[0] - 1):
        moved = ends_ref[s, 0:1, :] * start + ends_ref[s, 1:2, :]
        start = jnp.where(s < mine, moved, start)
    enthalpy = gain_ref[...] * start + shift_ref[...]
    enthalpy_ref[...] = enthalpy
    lane_iota = lax.broadcasted_iota(jnp.int32, (LANES, tubes), 0)
    total = jnp.zeros((slot_rows, 3 * LANES), F32)
    before = start
    for i in range(rows):
        after = enthalpy[i : i + 1, :]
        flow = after - before
        before = after
        where_row, where_lane = slot_parts(slots_ref[i : i + 1, :], cap, devices)
        hot = one_hot(where_row, slot_rows)
        chosen = lane_iota == where_lane
        spread = jnp.concatenate(
            [jnp.where(chosen, part.astype(F32), 0.0).astype(BF16) for part in pieces_of(flow, 3)], axis=0
        )
        total = total + lax.dot_general(hot, spread, (((1,), (1,)), ((), ())), preferred_element_type=F32)
    placed = total[:, :LANES] + total[:, LANES : 2 * LANES] + total[:, 2 * LANES :]
    for k in range(chunks):
        out_ref[:, k * LANES : (k + 1) * LANES] = placed[k * devices : (k + 1) * devices]


def march(ends, inlet, gain, shift, slots, cap, devices):
    return pl.pallas_call(
        functools.partial(march_kernel, "seg", cap, devices),
        out_shape=[
            jax.ShapeDtypeStruct(slots.shape, F32),
            jax.ShapeDtypeStruct((devices, cap), F32),
        ],
        compiler_params=pltpu.CompilerParams(vmem_limit_bytes=VMEM_LIMIT),
    )(ends, inlet[None], gain, shift, slots)


def deposit_kernel(flow_ref, cells_ref, fresh_ref, out_ref, total_ref):
    _, nx, ny, nz = fresh_ref.shape
    plane = nx * ny
    chunks = nz // LANES
    step = pl.program_id(0)
    where_row, where_lane = cell_parts(cells_ref[0, pl.ds(step, 1), :], plane, nz)
    cap = where_row.shape[1]
    hot = one_hot(where_row, plane * chunks)
    lane_iota = lax.broadcasted_iota(jnp.int32, (LANES, cap), 0)
    chosen = lane_iota == where_lane
    flow = flow_ref[pl.ds(step, 1), :]
    spread = jnp.concatenate(
        [jnp.where(chosen, part.astype(F32), 0.0).astype(BF16) for part in pieces_of(flow, 2)], axis=0
    )
    added = lax.dot_general(hot, spread, (((1,), (1,)), ((), ())), preferred_element_type=F32)

    @pl.when(step == 0)
    def _():
        total_ref[...] = added

    @pl.when(step > 0)
    def _():
        total_ref[...] += added

    @pl.when(step == pl.num_programs(0) - 1)
    def _():
        for k in range(chunks):
            lanes = slice(k * LANES, (k + 1) * LANES)
            rows = slice(k * plane, (k + 1) * plane)
            deposit = total_ref[rows, :LANES] + total_ref[rows, LANES:]
            out_ref[0, :, :, lanes] = fresh_ref[0, :, :, lanes] - DEPOSIT_SCALE * deposit.reshape(nx, ny, LANES)


def deposit(flow, wall_cells, fresh):
    devices, cap = flow.shape
    _, nx, ny, nz = fresh.shape
    block = pl.BlockSpec((1, nx, ny, nz), lambda i: (0, 0, 0, 0))
    return pl.pallas_call(
        deposit_kernel,
        grid=(devices,),
        in_specs=[
            pl.BlockSpec(flow.shape, lambda i: (0, 0)),
            pl.BlockSpec(wall_cells.shape, lambda i: (0, 0, 0)),
            block,
        ],
        out_specs=block,
        out_shape=jax.ShapeDtypeStruct(fresh.shape, F32),
        scratch_shapes=[pltpu.VMEM((nx * ny * nz // LANES, 2 * LANES), F32)],
        input_output_aliases={2: 0},
        compiler_params=pltpu.CompilerParams(vmem_limit_bytes=VMEM_LIMIT),
    )(flow, wall_cells, fresh)


def body(shell_state, diffusivity, inlet_enthalpy, transfer_units, wall_cells, tube_slots):
    _, devices, cap = wall_cells.shape
    fresh, outgoing = serve(shell_state, diffusivity, halo(shell_state), wall_cells)
    walls = lax.all_to_all(outgoing, ("tile", "seg"), split_axis=0, concat_axis=0, tiled=True)
    gain, shift, ends = lookup(walls, tube_slots, transfer_units)
    all_ends = lax.all_gather(ends, "seg")
    enthalpy, outbound = march(all_ends, inlet_enthalpy, gain, shift, tube_slots, cap, devices)
    flow = lax.all_to_all(outbound, ("tile", "seg"), split_axis=0, concat_axis=0, tiled=True)
    return deposit(flow, wall_cells, fresh), enthalpy


def solution(mesh):
    in_specs = (
        P(None, "tile", "seg", None),
        P("tile", "seg", None),
        P("tile"),
        P("seg", "tile"),
        P(("tile", "seg"), None, None),
        P("seg", "tile"),
    )
    out_specs = (P(None, "tile", "seg", None), P("seg", "tile"))
    return jax.shard_map(body, mesh=mesh, in_specs=in_specs, out_specs=out_specs, check_vma=False)
```

```python
import jax
import jax.numpy as jnp
from jax import lax
from jax.experimental import pallas as pl
from jax.experimental.pallas import tpu as pltpu
from jax.sharding import PartitionSpec as P

DEPOSIT_SCALE = 2.0
LANES = 128
BF16 = jnp.bfloat16
F32 = jnp.float32
MESH = pl.DeviceIdType.MESH
VMEM_LIMIT = 56 * 1024 * 1024


def pieces_of(value, count):
    parts = []
    for _ in range(count):
        part = value.astype(BF16)
        parts.append(part)
        value = value - part.astype(F32)
    return parts


def one_hot(index_row, rows):
    rows_iota = lax.broadcasted_iota(jnp.int32, (rows, index_row.shape[1]), 0)
    return jnp.where(rows_iota == index_row, 1.0, 0.0).astype(BF16)


def halo_kernel(state_ref, xl_ref, xh_ref, yl_ref, yh_ref, send_sems, recv_sems):
    tile, seg = lax.axis_index("tile"), lax.axis_index("seg")
    tiles, segs = lax.axis_size("tile"), lax.axis_size("seg")
    _, nx, ny, _ = state_ref.shape
    barrier = pltpu.get_barrier_semaphore()
    sides = (
        (tile + 1 < tiles, (tile + 1, seg), state_ref.at[:, nx - 1], xl_ref, xh_ref, 0, 1),
        (tile > 0, (tile - 1, seg), state_ref.at[:, 0], xh_ref, xl_ref, 1, 0),
        (seg + 1 < segs, (tile, seg + 1), state_ref.at[:, :, ny - 1], yl_ref, yh_ref, 2, 3),
        (seg > 0, (tile, seg - 1), state_ref.at[:, :, 0], yh_ref, yl_ref, 3, 2),
    )

    def copy_of(side):
        _, device, source, there, _, number, _ = side
        return pltpu.make_async_remote_copy(
            src_ref=source,
            dst_ref=there,
            send_sem=send_sems.at[number],
            recv_sem=recv_sems.at[number],
            device_id=device,
            device_id_type=MESH,
        )

    for side in sides:

        @pl.when(side[0])
        def _():
            pl.semaphore_signal(barrier, inc=1, device_id=side[1], device_id_type=MESH)

        @pl.when(jnp.logical_not(side[0]))
        def _():
            side[4][...] = jnp.zeros_like(side[4])

    pl.semaphore_wait(barrier, sum(side[0].astype(jnp.int32) for side in sides))

    for side in sides:

        @pl.when(side[0])
        def _():
            copy_of(side).start()

    for side in sides:

        @pl.when(side[0])
        def _():
            copy_of(side).wait_send()
            pltpu.make_async_copy(side[4], side[4], recv_sems.at[side[6]]).wait()


def halo(state):
    _, nx, ny, nz = state.shape
    vmem = pl.BlockSpec(memory_space=pltpu.VMEM)
    return pl.pallas_call(
        halo_kernel,
        in_specs=[pl.BlockSpec(memory_space=pl.ANY)],
        out_specs=[vmem] * 4,
        out_shape=[jax.ShapeDtypeStruct((4, n, nz), F32) for n in (ny, ny, nx, nx)],
        scratch_shapes=[pltpu.SemaphoreType.DMA((4,)), pltpu.SemaphoreType.DMA((4,))],
        compiler_params=pltpu.CompilerParams(
            collective_id=0, has_side_effects=True, vmem_limit_bytes=VMEM_LIMIT
        ),
    )(state)


def cell_parts(cells, plane, depth):
    xy = cells // depth
    z = cells % depth
    return (z // LANES) * plane + xy, z % LANES


def serve_kernel(
    state_ref, diff_ref, xl_ref, xh_ref, yl_ref, yh_ref, cells_ref,
    fresh_ref, out_ref, speed_ref, table_ref,
):
    nx, ny, nz = diff_ref.shape
    plane = nx * ny
    chunks = nz // LANES
    step = pl.program_id(0)

    @pl.when(step == 0)
    def _():
        row = lax.broadcasted_iota(jnp.int32, (ny, nz), 0)
        col = lax.broadcasted_iota(jnp.int32, (ny, nz), 1)

        def at_x(x, below, above):
            diffusivity = diff_ref[x]
            speed = None
            for c in range(4):
                cur = state_ref[c, x]
                nbr = above(c) + below(c)
                y_up = jnp.where(row == ny - 1, yh_ref[c, pl.ds(x, 1), :], pltpu.roll(cur, ny - 1, 0))
                y_dn = jnp.where(row == 0, yl_ref[c, pl.ds(x, 1), :], pltpu.roll(cur, 1, 0))
                nbr = nbr + y_up + y_dn
                z_up = jnp.where(col == nz - 1, 0.0, pltpu.roll(cur, nz - 1, 1))
                z_dn = jnp.where(col == 0, 0.0, pltpu.roll(cur, 1, 1))
                nbr = nbr + z_up + z_dn
                new = cur + diffusivity * (nbr - 6.0 * cur)
                fresh_ref[c, x] = new
                if c == 1:
                    speed = new * new
                elif c > 1:
                    speed = speed + new * new
            speed_ref[x] = speed

        at_x(0, lambda c: xl_ref[c], lambda c: state_ref[c, 1])

        def inner(x, carry):
            at_x(x, lambda c: state_ref[c, x - 1], lambda c: state_ref[c, x + 1])
            return carry

        lax.fori_loop(1, nx - 1, inner, 0)
        at_x(nx - 1, lambda c: state_ref[c, nx - 2], lambda c: xh_ref[c])

        for k in range(chunks):
            lanes = slice(k * LANES, (k + 1) * LANES)
            rows = slice(k * plane, (k + 1) * plane)
            for c in range(2):
                source = fresh_ref.at[0] if c == 0 else speed_ref
                block = source[:, :, lanes].reshape(plane, LANES)
                for p, part in enumerate(pieces_of(block.T, 2)):
                    base = (c * 2 + p) * LANES
                    table_ref[base : base + LANES, rows] = part

    where_row, where_lane = cell_parts(cells_ref[0, pl.ds(step, 1), :], plane, nz)
    cap = where_row.shape[1]
    hot = one_hot(where_row, plane * chunks)
    lines = jnp.dot(table_ref[...], hot, preferred_element_type=F32)
    lane_iota = lax.broadcasted_iota(jnp.int32, (LANES, cap), 0)
    chosen = lane_iota == where_lane
    for c in range(2):
        both = lines[2 * c * LANES : (2 * c + 1) * LANES] + lines[(2 * c + 1) * LANES : (2 * c + 2) * LANES]
        out_ref[0, c : c + 1, :] = jnp.sum(jnp.where(chosen, both, 0.0), axis=0, keepdims=True)


def serve(state, diffusivity, halos, wall_cells):
    _, devices, cap = wall_cells.shape
    nx, ny, nz = diffusivity.shape

    def whole(shape):
        return pl.BlockSpec(shape, lambda i: (0,) * len(shape))

    return pl.pallas_call(
        serve_kernel,
        grid=(devices,),
        in_specs=[whole(a.shape) for a in (state, diffusivity, *halos, wall_cells)],
        out_specs=[whole(state.shape), pl.BlockSpec((1, 2, cap), lambda i: (i, 0, 0))],
        out_shape=[
            jax.ShapeDtypeStruct(state.shape, F32),
            jax.ShapeDtypeStruct((devices, 2, cap), F32),
        ],
        scratch_shapes=[
            pltpu.VMEM((nx, ny, nz), F32),
            pltpu.VMEM((4 * LANES, nx * ny * nz // LANES), BF16),
        ],
        compiler_params=pltpu.CompilerParams(vmem_limit_bytes=VMEM_LIMIT),
    )(state, diffusivity, *halos, wall_cells)


def slot_parts(slots, cap, devices):
    owner = slots // cap
    column = slots % cap
    return (column // LANES) * devices + owner, column % LANES


def exchange_kernel(
    walls_ref, slots_ref, units_ref, inlet_ref, enthalpy_ref, flow_ref,
    walls_in, ends, outbound, table, gains, shifts, send_sems, recv_sems,
):
    devices, _, cap = walls_ref.shape
    rows, tubes = slots_ref.shape
    chunks = cap // LANES
    slot_rows = devices * chunks
    segs = lax.axis_size("seg")
    tile, seg = lax.axis_index("tile"), lax.axis_index("seg")
    me = tile * segs + seg

    def device(number):
        return (number // segs, number % segs)

    def send(source, there, phase, to):
        pltpu.make_async_remote_copy(
            src_ref=source,
            dst_ref=there,
            send_sem=send_sems.at[phase],
            recv_sem=recv_sems.at[phase],
            device_id=to,
            device_id_type=MESH,
        ).start()

    def wait_for(ref, sem):
        pltpu.make_async_copy(ref, ref, sem).wait()

    barrier = pltpu.get_barrier_semaphore()

    def greet(j, carry):
        pl.semaphore_signal(barrier, inc=1, device_id=device((me + j) % devices), device_id_type=MESH)
        return carry

    lax.fori_loop(1, devices, greet, 0)
    walls_in[me] = walls_ref[me]
    pl.semaphore_wait(barrier, devices - 1)

    def push_walls(j, carry):
        peer = (me + j) % devices
        send(walls_ref.at[peer], walls_in.at[me], 0, device(peer))
        return carry

    lax.fori_loop(1, devices, push_walls, 0)
    wait_for(walls_in.at[0 : devices - 1], recv_sems.at[0])

    for k in range(chunks):
        for c in range(2):
            block = walls_in[:, c, k * LANES : (k + 1) * LANES]
            for p, part in enumerate(pieces_of(block.T, 3)):
                first = p * slot_rows + k * devices
                table[c * LANES : (c + 1) * LANES, first : first + devices] = part
    lane_iota = lax.broadcasted_iota(jnp.int32, (LANES, tubes), 0)
    gain = jnp.ones((1, tubes), F32)
    shift = jnp.zeros((1, tubes), F32)
    for i in range(rows):
        where_row, where_lane = slot_parts(slots_ref[i : i + 1, :], cap, devices)
        hot = one_hot(where_row, slot_rows)
        hot = jnp.concatenate([hot, hot, hot], axis=0)
        lines = jnp.dot(table[...], hot, preferred_element_type=F32)
        chosen = lane_iota == where_lane
        temperature, speed = [
            jnp.sum(jnp.where(chosen, lines[c * LANES : (c + 1) * LANES], 0.0), axis=0, keepdims=True)
            for c in range(2)
        ]
        decay = jnp.exp(-units_ref[i : i + 1, :] * jnp.exp(0.3 * jnp.log(1.0 + speed)))
        source = (1.0 - decay) * temperature
        shift = decay * shift + source
        gain = decay * gain
        gains[i : i + 1, :] = gain
        shifts[i : i + 1, :] = shift
    ends[seg] = jnp.concatenate([gain, shift], axis=0)

    for j in range(1, segs):
        send(ends.at[seg], ends.at[seg], 1, (tile, (seg + j) % segs))
    wait_for(ends.at[0 : segs - 1], recv_sems.at[1])

    start = inlet_ref[...]
    for s in range(segs - 1):
        moved = ends[s, 0:1, :] * start + ends[s, 1:2, :]
        start = jnp.where(s < seg, moved, start)
    total = jnp.zeros((slot_rows, 3 * LANES), F32)
    before = start
    for i in range(rows):
        after = gains[i : i + 1, :] * start + shifts[i : i + 1, :]
        enthalpy_ref[i : i + 1, :] = after
        flow = after - before
        before = after
        where_row, where_lane = slot_parts(slots_ref[i : i + 1, :], cap, devices)
        hot = one_hot(where_row, slot_rows)
        chosen = lane_iota == where_lane
        spread = jnp.concatenate(
            [jnp.where(chosen, part.astype(F32), 0.0).astype(BF16) for part in pieces_of(flow, 3)], axis=0
        )
        total = total + lax.dot_general(hot, spread, (((1,), (1,)), ((), ())), preferred_element_type=F32)
    placed = total[:, :LANES] + total[:, LANES : 2 * LANES] + total[:, 2 * LANES :]
    for k in range(chunks):
        outbound[:, 0, k * LANES : (k + 1) * LANES] = placed[k * devices : (k + 1) * devices]

    def push_flow(j, carry):
        peer = (me + j) % devices
        send(outbound.at[peer], flow_ref.at[me], 2, device(peer))
        return carry

    lax.fori_loop(1, devices, push_flow, 0)
    flow_ref[me] = outbound[me]
    wait_for(walls_in.at[0 : devices - 1], send_sems.at[0])
    wait_for(ends.at[0 : segs - 1], send_sems.at[1])
    wait_for(flow_ref.at[0 : devices - 1], send_sems.at[2])
    wait_for(flow_ref.at[0 : devices - 1], recv_sems.at[2])


def exchange(outgoing, slots, units, inlet):
    devices, _, cap = outgoing.shape
    tubes = slots.shape[1]
    vmem = pl.BlockSpec(memory_space=pltpu.VMEM)
    return pl.pallas_call(
        exchange_kernel,
        in_specs=[vmem] * 4,
        out_specs=[vmem] * 2,
        out_shape=[
            jax.ShapeDtypeStruct(slots.shape, F32),
            jax.ShapeDtypeStruct((devices, 1, cap), F32),
        ],
        scratch_shapes=[
            pltpu.VMEM((devices, 2, cap), F32),
            pltpu.VMEM((lax.axis_size("seg"), 2, tubes), F32),
            pltpu.VMEM((devices, 1, cap), F32),
            pltpu.VMEM((2 * LANES, 3 * devices * cap // LANES), BF16),
            pltpu.VMEM(slots.shape, F32),
            pltpu.VMEM(slots.shape, F32),
            pltpu.SemaphoreType.DMA((3,)),
            pltpu.SemaphoreType.DMA((3,)),
        ],
        compiler_params=pltpu.CompilerParams(
            collective_id=1, has_side_effects=True, vmem_limit_bytes=VMEM_LIMIT
        ),
    )(outgoing, slots, units, inlet[None])


def deposit_kernel(flow_ref, cells_ref, fresh_ref, out_ref, total_ref):
    _, nx, ny, nz = fresh_ref.shape
    plane = nx * ny
    chunks = nz // LANES
    step = pl.program_id(0)
    where_row, where_lane = cell_parts(cells_ref[0, pl.ds(step, 1), :], plane, nz)
    cap = where_row.shape[1]
    hot = one_hot(where_row, plane * chunks)
    lane_iota = lax.broadcasted_iota(jnp.int32, (LANES, cap), 0)
    chosen = lane_iota == where_lane
    flow = flow_ref[step]
    spread = jnp.concatenate(
        [jnp.where(chosen, part.astype(F32), 0.0).astype(BF16) for part in pieces_of(flow, 2)], axis=0
    )
    added = lax.dot_general(hot, spread, (((1,), (1,)), ((), ())), preferred_element_type=F32)

    @pl.when(step == 0)
    def _():
        total_ref[...] = added

    @pl.when(step > 0)
    def _():
        total_ref[...] += added

    @pl.when(step == pl.num_programs(0) - 1)
    def _():
        for k in range(chunks):
            lanes = slice(k * LANES, (k + 1) * LANES)
            rows = slice(k * plane, (k + 1) * plane)
            deposit = total_ref[rows, :LANES] + total_ref[rows, LANES:]
            out_ref[0, :, :, lanes] = fresh_ref[0, :, :, lanes] - DEPOSIT_SCALE * deposit.reshape(nx, ny, LANES)


def deposit(flow, wall_cells, fresh):
    devices, _, cap = flow.shape
    _, nx, ny, nz = fresh.shape
    block = pl.BlockSpec((1, nx, ny, nz), lambda i: (0, 0, 0, 0))
    return pl.pallas_call(
        deposit_kernel,
        grid=(devices,),
        in_specs=[
            pl.BlockSpec(flow.shape, lambda i: (0, 0, 0)),
            pl.BlockSpec(wall_cells.shape, lambda i: (0, 0, 0)),
            block,
        ],
        out_specs=block,
        out_shape=jax.ShapeDtypeStruct(fresh.shape, F32),
        scratch_shapes=[pltpu.VMEM((nx * ny * nz // LANES, 2 * LANES), F32)],
        input_output_aliases={2: 0},
        compiler_params=pltpu.CompilerParams(vmem_limit_bytes=VMEM_LIMIT),
    )(flow, wall_cells, fresh)


def body(shell_state, diffusivity, inlet_enthalpy, transfer_units, wall_cells, tube_slots):
    fresh, outgoing = serve(shell_state, diffusivity, halo(shell_state), wall_cells)
    enthalpy, flow = exchange(outgoing, tube_slots, transfer_units, inlet_enthalpy)
    return deposit(flow, wall_cells, fresh), enthalpy


def solution(mesh):
    in_specs = (
        P(None, "tile", "seg", None),
        P("tile", "seg", None),
        P("tile"),
        P("seg", "tile"),
        P(("tile", "seg"), None, None),
        P("seg", "tile"),
    )
    out_specs = (P(None, "tile", "seg", None), P("seg", "tile"))
    return jax.shard_map(body, mesh=mesh, in_specs=in_specs, out_specs=out_specs, check_vma=False)
```

```python
import jax
import jax.numpy as jnp
from jax import lax
from jax.experimental import pallas as pl
from jax.experimental.pallas import tpu as pltpu
from jax.sharding import PartitionSpec as P

DEPOSIT_SCALE = 2.0
LANES = 128
GROUP = 4
BF16 = jnp.bfloat16
F32 = jnp.float32
MESH = pl.DeviceIdType.MESH
VMEM_LIMIT = 56 * 1024 * 1024


def pieces_of(value, count):
    parts = []
    for _ in range(count):
        part = value.astype(BF16)
        parts.append(part)
        value = value - part.astype(F32)
    return parts


def one_hot(index_row, rows):
    narrow = jnp.int16 if rows <= 32768 else jnp.int32
    rows_iota = lax.broadcasted_iota(jnp.int32, (rows, index_row.shape[1]), 0).astype(narrow)
    return jnp.where(rows_iota == index_row.astype(narrow), jnp.ones((), BF16), jnp.zeros((), BF16))


def cell_parts(cells, plane, depth):
    xy = cells // depth
    z = cells % depth
    return (z // LANES) * plane + xy, z % LANES


def slot_parts(slots, cap, devices):
    owner = slots // cap
    column = slots % cap
    return (column // LANES) * devices + owner, column % LANES


def march_kernel(
    state_ref, diff_ref, cells_ref, slots_ref, units_ref, inlet_ref,
    fresh_ref, enthalpy_ref, flow_ref,
    x_low, x_high, y_low, y_high, y_first, y_last, speed_field, cell_table,
    outgoing, walls_in, ends, outbound, flow_in, slot_table, gains, shifts,
    halo_send, halo_recv, send_sems, recv_sems,
):
    nx, ny, nz = diff_ref.shape
    plane = nx * ny
    step = pl.program_id(0)
    _, devices, cap = cells_ref.shape
    rows, tubes = slots_ref.shape
    slot_rows = devices * cap // LANES
    tiles, segs = lax.axis_size("tile"), lax.axis_size("seg")
    tile, seg = lax.axis_index("tile"), lax.axis_index("seg")
    me = tile * segs + seg
    peer = (me + step) % devices

    def device(number):
        return (number // segs, number % segs)

    def copy_of(source, there, send_sem, recv_sem, to):
        return pltpu.make_async_remote_copy(
            src_ref=source, dst_ref=there, send_sem=send_sem, recv_sem=recv_sem,
            device_id=to, device_id_type=MESH,
        )

    def send(source, there, phase, to):
        copy_of(source, there, send_sems.at[phase], recv_sems.at[phase], to).start()

    def wait_for(ref, sem):
        pltpu.make_async_copy(ref, ref, sem).wait()

    @pl.when(step == 0)
    def _():
        barrier = pltpu.get_barrier_semaphore()

        def greet(j, carry):
            pl.semaphore_signal(barrier, inc=1, device_id=device((me + j) % devices), device_id_type=MESH)
            return carry

        lax.fori_loop(1, devices, greet, 0)
        for c in range(4):
            for x in range(nx):
                y_first[c, x : x + 1, :] = state_ref[c, x, 0:1, :]
                y_last[c, x : x + 1, :] = state_ref[c, x, ny - 1 : ny, :]
        sides = (
            (tile + 1 < tiles, (tile + 1, seg), state_ref.at[:, nx - 1], x_low, x_high, 0, 1),
            (tile > 0, (tile - 1, seg), state_ref.at[:, 0], x_high, x_low, 1, 0),
            (seg + 1 < segs, (tile, seg + 1), y_last, y_low, y_high, 2, 3),
            (seg > 0, (tile, seg - 1), y_first, y_high, y_low, 3, 2),
        )
        pl.semaphore_wait(barrier, devices - 1)
        for side in sides:

            @pl.when(side[0])
            def _():
                copy_of(side[2], side[3], halo_send.at[side[5]], halo_recv.at[side[5]], side[1]).start()

            @pl.when(jnp.logical_not(side[0]))
            def _():
                side[4][...] = jnp.zeros_like(side[4])

        for side in sides:

            @pl.when(side[0])
            def _():
                wait_for(side[4], halo_recv.at[side[6]])
                wait_for(side[4], halo_send.at[side[5]])

        chunks = nz // LANES
        row = lax.broadcasted_iota(jnp.int32, (ny, nz), 0)
        col = lax.broadcasted_iota(jnp.int32, (ny, nz), 1)

        def at_x(x, below, above):
            diffusivity = diff_ref[x]
            speed = None
            for c in range(4):
                cur = state_ref[c, x]
                nbr = above(c) + below(c)
                y_up = jnp.where(row == ny - 1, y_high[c, pl.ds(x, 1), :], pltpu.roll(cur, ny - 1, 0))
                y_dn = jnp.where(row == 0, y_low[c, pl.ds(x, 1), :], pltpu.roll(cur, 1, 0))
                nbr = nbr + y_up + y_dn
                z_up = jnp.where(col == nz - 1, 0.0, pltpu.roll(cur, nz - 1, 1))
                z_dn = jnp.where(col == 0, 0.0, pltpu.roll(cur, 1, 1))
                nbr = nbr + z_up + z_dn
                new = cur + diffusivity * (nbr - 6.0 * cur)
                fresh_ref[c, x] = new
                if c == 1:
                    speed = new * new
                elif c > 1:
                    speed = speed + new * new
            speed_field[x] = speed

        at_x(0, lambda c: x_low[c], lambda c: state_ref[c, 1])

        def inner(x, carry):
            at_x(x, lambda c: state_ref[c, x - 1], lambda c: state_ref[c, x + 1])
            return carry

        lax.fori_loop(1, nx - 1, inner, 0)
        at_x(nx - 1, lambda c: state_ref[c, nx - 2], lambda c: x_high[c])

        for k in range(chunks):
            lanes = slice(k * LANES, (k + 1) * LANES)
            rows = slice(k * plane, (k + 1) * plane)
            for c in range(2):
                source = fresh_ref.at[0] if c == 0 else speed_field
                block = source[:, :, lanes].reshape(plane, LANES)
                for p, part in enumerate(pieces_of(block.T, 2)):
                    base = (c * 2 + p) * LANES
                    cell_table[base : base + LANES, rows] = part

    where_row, where_lane = cell_parts(cells_ref[0, pl.ds(peer, 1), :], plane, nz)
    hot = one_hot(where_row, plane * (nz // LANES))
    lines = jnp.dot(cell_table[...], hot, preferred_element_type=F32)
    chosen = lax.broadcasted_iota(jnp.int32, (LANES, cap), 0) == where_lane
    picked = []
    for c in range(2):
        both = lines[2 * c * LANES : (2 * c + 1) * LANES] + lines[(2 * c + 1) * LANES : (2 * c + 2) * LANES]
        picked.append(jnp.sum(jnp.where(chosen, both, 0.0), axis=0, keepdims=True))
    picked = jnp.concatenate(picked, axis=0)

    @pl.when(step == 0)
    def _():
        walls_in[me] = picked

    @pl.when(step > 0)
    def _():
        outgoing[peer] = picked
        send(outgoing.at[peer], walls_in.at[me], 0, device(peer))

    @pl.when(step == devices - 1)
    def _():
        chunks = cap // LANES
        wait_for(walls_in.at[0 : devices - 1], recv_sems.at[0])
        for k in range(chunks):
            for c in range(2):
                block = walls_in[:, c, k * LANES : (k + 1) * LANES]
                for p, part in enumerate(pieces_of(block.T, 3)):
                    first = p * slot_rows + k * devices
                    slot_table[c * LANES : (c + 1) * LANES, first : first + devices] = part
        lane_iota = lax.broadcasted_iota(jnp.int32, (LANES, tubes), 0)
        gain = jnp.ones((1, tubes), F32)
        shift = jnp.zeros((1, tubes), F32)
        for i in range(rows):
            where_row, where_lane = slot_parts(slots_ref[i : i + 1, :], cap, devices)
            hot = one_hot(where_row, slot_rows)
            hot = jnp.concatenate([hot, hot, hot], axis=0)
            lines = jnp.dot(slot_table[...], hot, preferred_element_type=F32)
            chosen = lane_iota == where_lane
            temperature, speed = [
                jnp.sum(jnp.where(chosen, lines[c * LANES : (c + 1) * LANES], 0.0), axis=0, keepdims=True)
                for c in range(2)
            ]
            decay = jnp.exp(-units_ref[i : i + 1, :] * jnp.exp(0.3 * jnp.log(1.0 + speed)))
            source = (1.0 - decay) * temperature
            shift = decay * shift + source
            gain = decay * gain
            gains[i : i + 1, :] = gain
            shifts[i : i + 1, :] = shift
        ends[seg] = jnp.concatenate([gain, shift], axis=0)

        for j in range(1, segs):
            send(ends.at[seg], ends.at[seg], 1, (tile, (seg + j) % segs))
        wait_for(ends.at[0 : segs - 1], recv_sems.at[1])

        start = inlet_ref[...]
        for s in range(segs - 1):
            moved = ends[s, 0:1, :] * start + ends[s, 1:2, :]
            start = jnp.where(s < seg, moved, start)
        total = jnp.zeros((slot_rows, 3 * LANES), F32)
        before = start
        for i in range(rows):
            after = gains[i : i + 1, :] * start + shifts[i : i + 1, :]
            enthalpy_ref[i : i + 1, :] = after
            flow = after - before
            before = after
            where_row, where_lane = slot_parts(slots_ref[i : i + 1, :], cap, devices)
            hot = one_hot(where_row, slot_rows)
            chosen = lane_iota == where_lane
            spread = jnp.concatenate(
                [jnp.where(chosen, part.astype(F32), 0.0).astype(BF16) for part in pieces_of(flow, 3)], axis=0
            )
            total = total + lax.dot_general(hot, spread, (((1,), (1,)), ((), ())), preferred_element_type=F32)
        placed = total[:, :LANES] + total[:, LANES : 2 * LANES] + total[:, 2 * LANES :]
        for k in range(chunks):
            outbound[:, 0, k * LANES : (k + 1) * LANES] = placed[k * devices : (k + 1) * devices]

        def push_flow(j, carry):
            peer = (me + j) % devices
            send(outbound.at[peer], flow_in.at[me], 2, device(peer))
            return carry

        lax.fori_loop(1, devices, push_flow, 0)
        flow_in[me] = outbound[me]
        wait_for(outgoing.at[0 : devices - 1], send_sems.at[0])
        wait_for(ends.at[0 : segs - 1], send_sems.at[1])
        wait_for(outbound.at[0 : devices - 1], send_sems.at[2])
        wait_for(flow_in.at[0 : devices - 1], recv_sems.at[2])
        flow_ref[...] = flow_in[...]


def march(state, diffusivity, wall_cells, slots, units, inlet):
    _, devices, cap = wall_cells.shape
    nx, ny, nz = diffusivity.shape
    rows, tubes = slots.shape
    ins = (state, diffusivity, wall_cells, slots, units, inlet[None])
    outs = (state.shape, slots.shape, (devices, 1, cap))

    def whole(shape):
        return pl.BlockSpec(shape, lambda i: (0,) * len(shape))

    return pl.pallas_call(
        march_kernel,
        grid=(devices,),
        in_specs=[whole(a.shape) for a in ins],
        out_specs=[whole(shape) for shape in outs],
        out_shape=[jax.ShapeDtypeStruct(shape, F32) for shape in outs],
        scratch_shapes=[
            pltpu.VMEM((4, ny, nz), F32),
            pltpu.VMEM((4, ny, nz), F32),
            pltpu.VMEM((4, nx, nz), F32),
            pltpu.VMEM((4, nx, nz), F32),
            pltpu.VMEM((4, nx, nz), F32),
            pltpu.VMEM((4, nx, nz), F32),
            pltpu.VMEM((nx, ny, nz), F32),
            pltpu.VMEM((4 * LANES, nx * ny * nz // LANES), BF16),
            pltpu.VMEM((devices, 2, cap), F32),
            pltpu.VMEM((devices, 2, cap), F32),
            pltpu.VMEM((lax.axis_size("seg"), 2, tubes), F32),
            pltpu.VMEM((devices, 1, cap), F32),
            pltpu.VMEM((devices, 1, cap), F32),
            pltpu.VMEM((2 * LANES, 3 * devices * cap // LANES), BF16),
            pltpu.VMEM((rows, tubes), F32),
            pltpu.VMEM((rows, tubes), F32),
            pltpu.SemaphoreType.DMA((4,)),
            pltpu.SemaphoreType.DMA((4,)),
            pltpu.SemaphoreType.DMA((3,)),
            pltpu.SemaphoreType.DMA((3,)),
        ],
        compiler_params=pltpu.CompilerParams(
            collective_id=0, has_side_effects=True, vmem_limit_bytes=VMEM_LIMIT
        ),
    )(*ins)


def deposit_kernel(flow_ref, cells_ref, fresh_ref, out_ref, total_ref):
    _, nx, ny, nz = fresh_ref.shape
    plane = nx * ny
    chunks = nz // LANES
    step = pl.program_id(0)
    cap = flow_ref.shape[2]
    lane_iota = lax.broadcasted_iota(jnp.int32, (LANES, cap), 0)
    hots, spreads = [], []
    for j in range(GROUP):
        owner = step * GROUP + j
        where_row, where_lane = cell_parts(cells_ref[0, pl.ds(owner, 1), :], plane, nz)
        chosen = lane_iota == where_lane
        parts = [jnp.where(chosen, part.astype(F32), 0.0).astype(BF16) for part in pieces_of(flow_ref[owner], 2)]
        hots.append(one_hot(where_row, plane * chunks))
        spreads.append(jnp.concatenate(parts, axis=0))
    added = lax.dot_general(
        jnp.concatenate(hots, axis=1),
        jnp.concatenate(spreads, axis=1),
        (((1,), (1,)), ((), ())),
        preferred_element_type=F32,
    )

    @pl.when(step == 0)
    def _():
        total_ref[...] = added

    @pl.when(step > 0)
    def _():
        total_ref[...] += added

    @pl.when(step == pl.num_programs(0) - 1)
    def _():
        for k in range(chunks):
            lanes = slice(k * LANES, (k + 1) * LANES)
            rows = slice(k * plane, (k + 1) * plane)
            deposit = total_ref[rows, :LANES] + total_ref[rows, LANES:]
            out_ref[0, :, :, lanes] = fresh_ref[0, :, :, lanes] - DEPOSIT_SCALE * deposit.reshape(nx, ny, LANES)


def deposit(flow, wall_cells, fresh):
    devices, _, cap = flow.shape
    _, nx, ny, nz = fresh.shape
    block = pl.BlockSpec((1, nx, ny, nz), lambda i: (0, 0, 0, 0))
    return pl.pallas_call(
        deposit_kernel,
        grid=(devices // GROUP,),
        in_specs=[
            pl.BlockSpec(flow.shape, lambda i: (0, 0, 0)),
            pl.BlockSpec(wall_cells.shape, lambda i: (0, 0, 0)),
            block,
        ],
        out_specs=block,
        out_shape=jax.ShapeDtypeStruct(fresh.shape, F32),
        scratch_shapes=[pltpu.VMEM((nx * ny * nz // LANES, 2 * LANES), F32)],
        input_output_aliases={2: 0},
        compiler_params=pltpu.CompilerParams(vmem_limit_bytes=VMEM_LIMIT),
    )(flow, wall_cells, fresh)


def body(shell_state, diffusivity, inlet_enthalpy, transfer_units, wall_cells, tube_slots):
    fresh, enthalpy, flow = march(
        shell_state, diffusivity, wall_cells, tube_slots, transfer_units, inlet_enthalpy
    )
    return deposit(flow, wall_cells, fresh), enthalpy


def solution(mesh):
    in_specs = (
        P(None, "tile", "seg", None),
        P("tile", "seg", None),
        P("tile"),
        P("seg", "tile"),
        P(("tile", "seg"), None, None),
        P("seg", "tile"),
    )
    out_specs = (P(None, "tile", "seg", None), P("seg", "tile"))
    return jax.shard_map(body, mesh=mesh, in_specs=in_specs, out_specs=out_specs, check_vma=False)
```

```python
import jax
import jax.numpy as jnp
from jax import lax
from jax.experimental import pallas as pl
from jax.experimental.pallas import tpu as pltpu
from jax.sharding import PartitionSpec as P

DEPOSIT_SCALE = 2.0
LANES = 128
GROUP = 4
PAIR = 2
BF16 = jnp.bfloat16
F32 = jnp.float32
MESH = pl.DeviceIdType.MESH
VMEM_LIMIT = 56 * 1024 * 1024


def pieces_of(value, count):
    parts = []
    for _ in range(count):
        part = value.astype(BF16)
        parts.append(part)
        value = value - part.astype(F32)
    return parts


def one_hot(index_row, rows):
    narrow = jnp.int16 if rows <= 32768 else jnp.int32
    rows_iota = lax.broadcasted_iota(jnp.int32, (rows, index_row.shape[1]), 0).astype(narrow)
    return jnp.where(rows_iota == index_row.astype(narrow), jnp.ones((), BF16), jnp.zeros((), BF16))


def cell_parts(cells, plane, depth):
    xy = cells // depth
    z = cells % depth
    return (z // LANES) * plane + xy, z % LANES


def slot_parts(slots, cap, devices):
    owner = slots // cap
    column = slots % cap
    return (column // LANES) * devices + owner, column % LANES


def march_kernel(
    state_ref, diff_ref, cells_ref, slots_ref, units_ref, inlet_ref,
    fresh_ref, enthalpy_ref, flow_ref,
    x_low, x_high, y_low, y_high, y_first, y_last, speed_field, cell_table,
    outgoing, walls_in, ends, outbound, flow_in, slot_table, gains, shifts,
    halo_send, halo_recv, send_sems, recv_sems,
):
    nx, ny, nz = diff_ref.shape
    plane = nx * ny
    step = pl.program_id(0)
    _, devices, cap = cells_ref.shape
    rows, tubes = slots_ref.shape
    slot_rows = devices * cap // LANES
    tiles, segs = lax.axis_size("tile"), lax.axis_size("seg")
    tile, seg = lax.axis_index("tile"), lax.axis_index("seg")
    me = tile * segs + seg
    peers = [(me + step * PAIR + u) % devices for u in range(PAIR)]

    def device(number):
        return (number // segs, number % segs)

    def copy_of(source, there, send_sem, recv_sem, to):
        return pltpu.make_async_remote_copy(
            src_ref=source, dst_ref=there, send_sem=send_sem, recv_sem=recv_sem,
            device_id=to, device_id_type=MESH,
        )

    def send(source, there, phase, to):
        copy_of(source, there, send_sems.at[phase], recv_sems.at[phase], to).start()

    def wait_for(ref, sem):
        pltpu.make_async_copy(ref, ref, sem).wait()

    @pl.when(step == 0)
    def _():
        barrier = pltpu.get_barrier_semaphore()

        def greet(j, carry):
            pl.semaphore_signal(barrier, inc=1, device_id=device((me + j) % devices), device_id_type=MESH)
            return carry

        lax.fori_loop(1, devices, greet, 0)
        for c in range(4):
            for x in range(nx):
                y_first[c, x : x + 1, :] = state_ref[c, x, 0:1, :]
                y_last[c, x : x + 1, :] = state_ref[c, x, ny - 1 : ny, :]
        sides = (
            (tile + 1 < tiles, (tile + 1, seg), state_ref.at[:, nx - 1], x_low, x_high, 0, 1),
            (tile > 0, (tile - 1, seg), state_ref.at[:, 0], x_high, x_low, 1, 0),
            (seg + 1 < segs, (tile, seg + 1), y_last, y_low, y_high, 2, 3),
            (seg > 0, (tile, seg - 1), y_first, y_high, y_low, 3, 2),
        )
        pl.semaphore_wait(barrier, devices - 1)
        for side in sides:

            @pl.when(side[0])
            def _():
                copy_of(side[2], side[3], halo_send.at[side[5]], halo_recv.at[side[5]], side[1]).start()

            @pl.when(jnp.logical_not(side[0]))
            def _():
                side[4][...] = jnp.zeros_like(side[4])

        for side in sides:

            @pl.when(side[0])
            def _():
                wait_for(side[4], halo_recv.at[side[6]])
                wait_for(side[4], halo_send.at[side[5]])

        chunks = nz // LANES
        row = lax.broadcasted_iota(jnp.int32, (ny, nz), 0)
        col = lax.broadcasted_iota(jnp.int32, (ny, nz), 1)

        def at_x(x, below, above):
            diffusivity = diff_ref[x]
            speed = None
            for c in range(4):
                cur = state_ref[c, x]
                nbr = above(c) + below(c)
                y_up = jnp.where(row == ny - 1, y_high[c, pl.ds(x, 1), :], pltpu.roll(cur, ny - 1, 0))
                y_dn = jnp.where(row == 0, y_low[c, pl.ds(x, 1), :], pltpu.roll(cur, 1, 0))
                nbr = nbr + y_up + y_dn
                z_up = jnp.where(col == nz - 1, 0.0, pltpu.roll(cur, nz - 1, 1))
                z_dn = jnp.where(col == 0, 0.0, pltpu.roll(cur, 1, 1))
                nbr = nbr + z_up + z_dn
                new = cur + diffusivity * (nbr - 6.0 * cur)
                fresh_ref[c, x] = new
                if c == 1:
                    speed = new * new
                elif c > 1:
                    speed = speed + new * new
            speed_field[x] = speed

        at_x(0, lambda c: x_low[c], lambda c: state_ref[c, 1])

        def inner(x, carry):
            at_x(x, lambda c: state_ref[c, x - 1], lambda c: state_ref[c, x + 1])
            return carry

        lax.fori_loop(1, nx - 1, inner, 0)
        at_x(nx - 1, lambda c: state_ref[c, nx - 2], lambda c: x_high[c])

        for k in range(chunks):
            lanes = slice(k * LANES, (k + 1) * LANES)
            rows = slice(k * plane, (k + 1) * plane)
            for c in range(2):
                source = fresh_ref.at[0] if c == 0 else speed_field
                block = source[:, :, lanes].reshape(plane, LANES)
                for p, part in enumerate(pieces_of(block.T, 2)):
                    base = (c * 2 + p) * LANES
                    cell_table[base : base + LANES, rows] = part

    blocks = []
    for peer in peers:
        where_row, where_lane = cell_parts(cells_ref[0, pl.ds(peer, 1), :], plane, nz)
        hot = one_hot(where_row, plane * (nz // LANES))
        lines = jnp.dot(cell_table[...], hot, preferred_element_type=F32)
        chosen = lax.broadcasted_iota(jnp.int32, (LANES, cap), 0) == where_lane
        picked = []
        for c in range(2):
            both = lines[2 * c * LANES : (2 * c + 1) * LANES] + lines[(2 * c + 1) * LANES : (2 * c + 2) * LANES]
            picked.append(jnp.sum(jnp.where(chosen, both, 0.0), axis=0, keepdims=True))
        blocks.append(jnp.concatenate(picked, axis=0))

    @pl.when(step == 0)
    def _():
        walls_in[me] = blocks[0]

    @pl.when(step > 0)
    def _():
        outgoing[peers[0]] = blocks[0]
        send(outgoing.at[peers[0]], walls_in.at[me], 0, device(peers[0]))

    for peer, block in zip(peers[1:], blocks[1:]):
        outgoing[peer] = block
        send(outgoing.at[peer], walls_in.at[me], 0, device(peer))

    @pl.when(step == devices // PAIR - 1)
    def _():
        chunks = cap // LANES
        wait_for(walls_in.at[0 : devices - 1], recv_sems.at[0])
        for k in range(chunks):
            for c in range(2):
                block = walls_in[:, c, k * LANES : (k + 1) * LANES]
                for p, part in enumerate(pieces_of(block.T, 3)):
                    first = p * slot_rows + k * devices
                    slot_table[c * LANES : (c + 1) * LANES, first : first + devices] = part
        lane_iota = lax.broadcasted_iota(jnp.int32, (LANES, tubes), 0)
        gain = jnp.ones((1, tubes), F32)
        shift = jnp.zeros((1, tubes), F32)
        for i in range(rows):
            where_row, where_lane = slot_parts(slots_ref[i : i + 1, :], cap, devices)
            hot = one_hot(where_row, slot_rows)
            hot = jnp.concatenate([hot, hot, hot], axis=0)
            lines = jnp.dot(slot_table[...], hot, preferred_element_type=F32)
            chosen = lane_iota == where_lane
            temperature, speed = [
                jnp.sum(jnp.where(chosen, lines[c * LANES : (c + 1) * LANES], 0.0), axis=0, keepdims=True)
                for c in range(2)
            ]
            decay = jnp.exp(-units_ref[i : i + 1, :] * jnp.exp(0.3 * jnp.log(1.0 + speed)))
            source = (1.0 - decay) * temperature
            shift = decay * shift + source
            gain = decay * gain
            gains[i : i + 1, :] = gain
            shifts[i : i + 1, :] = shift
        ends[seg] = jnp.concatenate([gain, shift], axis=0)

        for j in range(1, segs):
            send(ends.at[seg], ends.at[seg], 1, (tile, (seg + j) % segs))
        wait_for(ends.at[0 : segs - 1], recv_sems.at[1])

        start = inlet_ref[...]
        for s in range(segs - 1):
            moved = ends[s, 0:1, :] * start + ends[s, 1:2, :]
            start = jnp.where(s < seg, moved, start)
        total = jnp.zeros((slot_rows, 3 * LANES), F32)
        before = start
        for i in range(rows):
            after = gains[i : i + 1, :] * start + shifts[i : i + 1, :]
            enthalpy_ref[i : i + 1, :] = after
            flow = after - before
            before = after
            where_row, where_lane = slot_parts(slots_ref[i : i + 1, :], cap, devices)
            hot = one_hot(where_row, slot_rows)
            chosen = lane_iota == where_lane
            spread = jnp.concatenate(
                [jnp.where(chosen, part.astype(F32), 0.0).astype(BF16) for part in pieces_of(flow, 3)], axis=0
            )
            total = total + lax.dot_general(hot, spread, (((1,), (1,)), ((), ())), preferred_element_type=F32)
        placed = total[:, :LANES] + total[:, LANES : 2 * LANES] + total[:, 2 * LANES :]
        for k in range(chunks):
            outbound[:, 0, k * LANES : (k + 1) * LANES] = placed[k * devices : (k + 1) * devices]

        def push_flow(j, carry):
            peer = (me + j) % devices
            send(outbound.at[peer], flow_in.at[me], 2, device(peer))
            return carry

        lax.fori_loop(1, devices, push_flow, 0)
        flow_in[me] = outbound[me]
        wait_for(outgoing.at[0 : devices - 1], send_sems.at[0])
        wait_for(ends.at[0 : segs - 1], send_sems.at[1])
        wait_for(outbound.at[0 : devices - 1], send_sems.at[2])
        wait_for(flow_in.at[0 : devices - 1], recv_sems.at[2])
        flow_ref[...] = flow_in[...]


def march(state, diffusivity, wall_cells, slots, units, inlet):
    _, devices, cap = wall_cells.shape
    nx, ny, nz = diffusivity.shape
    rows, tubes = slots.shape
    ins = (state, diffusivity, wall_cells, slots, units, inlet[None])
    outs = (state.shape, slots.shape, (devices, 1, cap))

    def whole(shape):
        return pl.BlockSpec(shape, lambda i: (0,) * len(shape))

    return pl.pallas_call(
        march_kernel,
        grid=(devices // PAIR,),
        in_specs=[whole(a.shape) for a in ins],
        out_specs=[whole(shape) for shape in outs],
        out_shape=[jax.ShapeDtypeStruct(shape, F32) for shape in outs],
        scratch_shapes=[
            pltpu.VMEM((4, ny, nz), F32),
            pltpu.VMEM((4, ny, nz), F32),
            pltpu.VMEM((4, nx, nz), F32),
            pltpu.VMEM((4, nx, nz), F32),
            pltpu.VMEM((4, nx, nz), F32),
            pltpu.VMEM((4, nx, nz), F32),
            pltpu.VMEM((nx, ny, nz), F32),
            pltpu.VMEM((4 * LANES, nx * ny * nz // LANES), BF16),
            pltpu.VMEM((devices, 2, cap), F32),
            pltpu.VMEM((devices, 2, cap), F32),
            pltpu.VMEM((lax.axis_size("seg"), 2, tubes), F32),
            pltpu.VMEM((devices, 1, cap), F32),
            pltpu.VMEM((devices, 1, cap), F32),
            pltpu.VMEM((2 * LANES, 3 * devices * cap // LANES), BF16),
            pltpu.VMEM((rows, tubes), F32),
            pltpu.VMEM((rows, tubes), F32),
            pltpu.SemaphoreType.DMA((4,)),
            pltpu.SemaphoreType.DMA((4,)),
            pltpu.SemaphoreType.DMA((3,)),
            pltpu.SemaphoreType.DMA((3,)),
        ],
        compiler_params=pltpu.CompilerParams(
            collective_id=0, has_side_effects=True, vmem_limit_bytes=VMEM_LIMIT
        ),
    )(*ins)


def deposit_kernel(flow_ref, cells_ref, fresh_ref, rest_ref, out_ref, total_ref, heated_ref, sems):
    _, nx, ny, nz = fresh_ref.shape
    keep = pltpu.make_async_copy(rest_ref.at[1:4], out_ref.at[1:4], sems.at[0])
    plane = nx * ny
    chunks = nz // LANES
    step = pl.program_id(0)
    @pl.when(step == 0)
    def _():
        keep.start()

    cap = flow_ref.shape[2]
    lane_iota = lax.broadcasted_iota(jnp.int32, (LANES, cap), 0)
    hots, spreads = [], []
    for j in range(GROUP):
        owner = step * GROUP + j
        where_row, where_lane = cell_parts(cells_ref[0, pl.ds(owner, 1), :], plane, nz)
        chosen = lane_iota == where_lane
        parts = [jnp.where(chosen, part.astype(F32), 0.0).astype(BF16) for part in pieces_of(flow_ref[owner], 2)]
        hots.append(one_hot(where_row, plane * chunks))
        spreads.append(jnp.concatenate(parts, axis=0))
    added = lax.dot_general(
        jnp.concatenate(hots, axis=1),
        jnp.concatenate(spreads, axis=1),
        (((1,), (1,)), ((), ())),
        preferred_element_type=F32,
    )

    @pl.when(step == 0)
    def _():
        total_ref[...] = added

    @pl.when(step > 0)
    def _():
        total_ref[...] += added

    @pl.when(step == pl.num_programs(0) - 1)
    def _():
        for k in range(chunks):
            lanes = slice(k * LANES, (k + 1) * LANES)
            rows = slice(k * plane, (k + 1) * plane)
            deposit = total_ref[rows, :LANES] + total_ref[rows, LANES:]
            heated_ref[:, :, lanes] = fresh_ref[0, :, :, lanes] - DEPOSIT_SCALE * deposit.reshape(nx, ny, LANES)
        give = pltpu.make_async_copy(heated_ref, out_ref.at[0], sems.at[1])
        give.start()
        give.wait()
        keep.wait()


def deposit(flow, wall_cells, fresh):
    devices, _, cap = flow.shape
    _, nx, ny, nz = fresh.shape
    block = pl.BlockSpec((1, nx, ny, nz), lambda i: (0, 0, 0, 0))
    return pl.pallas_call(
        deposit_kernel,
        grid=(devices // GROUP,),
        in_specs=[
            pl.BlockSpec(flow.shape, lambda i: (0, 0, 0)),
            pl.BlockSpec(wall_cells.shape, lambda i: (0, 0, 0)),
            block,
            pl.BlockSpec(memory_space=pl.ANY),
        ],
        out_specs=pl.BlockSpec(memory_space=pl.ANY),
        out_shape=jax.ShapeDtypeStruct(fresh.shape, F32),
        scratch_shapes=[
            pltpu.VMEM((nx * ny * nz // LANES, 2 * LANES), F32),
            pltpu.VMEM((nx, ny, nz), F32),
            pltpu.SemaphoreType.DMA((2,)),
        ],
        compiler_params=pltpu.CompilerParams(vmem_limit_bytes=VMEM_LIMIT),
    )(flow, wall_cells, fresh, fresh)


def body(shell_state, diffusivity, inlet_enthalpy, transfer_units, wall_cells, tube_slots):
    fresh, enthalpy, flow = march(
        shell_state, diffusivity, wall_cells, tube_slots, transfer_units, inlet_enthalpy
    )
    return deposit(flow, wall_cells, fresh), enthalpy


def solution(mesh):
    in_specs = (
        P(None, "tile", "seg", None),
        P("tile", "seg", None),
        P("tile"),
        P("seg", "tile"),
        P(("tile", "seg"), None, None),
        P("seg", "tile"),
    )
    out_specs = (P(None, "tile", "seg", None), P("seg", "tile"))
    return jax.shard_map(body, mesh=mesh, in_specs=in_specs, out_specs=out_specs, check_vma=False)
```
